128 devices in a mesh: ctx: 32 (over z, y, core), head: 4 (over x).
Axes of the slice: x: 4, y: 4, z: 4, core: 2. Of those that a mesh axis runs over, the one named last changes fastest.
Arguments:
- queries: bfloat16 [49152, 2048], P('ctx', 'head'), may hold values from -20 to 20
- keys: bfloat16 [49152, 2048], P('ctx', 'head'), may hold values from -20 to 20
- values: bfloat16 [49152, 2048], P('ctx', 'head'), may hold values from -6 to 6
- offsets: int32 [3, 16], replicated, may hold values from 0 to 7, as said below
- out_weight: bfloat16 [2048, 2048], replicated, may hold values from -1.1953125 to 1.1953125
Outputs:
- mixed: bfloat16 [49152, 2048], P(('ctx', 'head'))
The draws below stay inside these ranges and needn't reach their ends.
Inputs may be any that keep to these rules, and one draw needn't show every extreme that they name: `offsets`: each offset of row k - 1 lies in 0 to 2^k - 1; in the last row every value of that range occurs.
All inputs are finite; a program needn't handle non-finite values.
Results may differ from the reference program's by a relative error of at most 0.0053.
Values may be sent and summed in bfloat16 or wider, within the bound.
A program may use at most 192 MiB of HBM per device.

```python
import math
import jax
import jax.numpy as jnp
from jax import lax

D = 2048
HEADS = 16
DH = 128
TOK_DEV = 1536
LEVELS = 4
L = 49152


def drawn(key, salt):
    return jnp.clip(jax.random.normal(jax.random.fold_in(key, salt), (L, D), jnp.float32), -4.0, 4.0)


def draw_queries(key, part):
    entries = drawn(key, 21)
    return entries.astype(jnp.bfloat16)


def draw_keys(key, part):
    entries = drawn(key, 23)
    return entries.astype(jnp.bfloat16)


def draw_offsets(key, part):
    listed = []
    for level_index in range(1, LEVELS):
        order = jax.random.permutation(jax.random.fold_in(key, 30 + level_index), HEADS)
        listed.append(order % 2 ** level_index)
    return jnp.stack(listed).astype(jnp.int32)


def block_levels(rng, extent, shards, low, high):
    def one(dim, blocks):
        draws = jax.random.uniform(jax.random.fold_in(jax.random.fold_in(rng, 6), dim), (blocks,), jnp.float32, low / len(shards), high / len(shards))
        return jnp.repeat(jnp.exp(draws), extent[dim] // blocks).reshape((-1,) + (1,) * (len(extent) - dim - 1))

    factor_of = one(*shards[0])
    for cut in shards[1:]:
        factor_of = factor_of * one(*cut)
    return factor_of


def bell_draw(own_key, dims, width, most, shards=(), held_as=jnp.bfloat16):
    factor_of = block_levels(own_key, dims, shards, -0.22, 0.18) if shards else 1.0
    drawn = jax.random.normal(own_key, dims, jnp.float32) * width * factor_of
    return jnp.minimum(jnp.maximum(drawn, -most), most).astype(held_as)


def setup_inputs(seed: int = 0) -> dict:
    seeds = jax.random.split(jax.random.key(seed), 6)
    return {
        "queries": draw_queries(jax.random.fold_in(seeds[5], 71), 0),
        "keys": draw_keys(jax.random.fold_in(seeds[5], 71), 0),
        "values": bell_draw(seeds[2], (L, D), 1.0, 6.0, ((0, 32), (1, 4))),
        "offsets": draw_offsets(jax.random.fold_in(seeds[5], 71), 0),
        "out_weight": bell_draw(seeds[4], (D, D), 0.2, 1.1953125),
    }


NEG_FILL = -1e+30

def attend_one(query_rows, key_rows, value_rows):
    number = query_rows.shape[0]
    scores = jnp.dot(query_rows, key_rows.T, preferred_element_type=jnp.float32) * (1.0 / math.sqrt(DH))
    index_rows = jnp.arange(number)
    scores = jnp.where(index_rows[:, None] >= index_rows[None, :], scores, NEG_FILL)
    row_max = lax.optimization_barrier(jnp.max(scores, axis=1))
    weights = jnp.exp(scores - row_max[:, None])
    row_sum = lax.optimization_barrier(jnp.sum(weights, axis=1))
    weighted = jnp.dot(weights.astype(jnp.bfloat16), value_rows, preferred_element_type=jnp.float32)
    return (row_max, row_sum, weighted)

def level_terms(query_heads, key_heads, value_heads, shifts, dilation):
    segments = query_heads.shape[0] // (TOK_DEV * dilation)
    hits = jnp.arange(dilation)[:, None] == shifts[None, :]

    def select(source):
        shaped = source.reshape(segments, TOK_DEV, dilation, HEADS, DH)
        return lax.optimization_barrier(jnp.sum(jnp.where(hits[None, None, :, :, None], shaped, jnp.zeros((), source.dtype)), axis=2))
    picked_q, picked_k, picked_v = (select(query_heads), select(key_heads), select(value_heads))

    def per_segment(items):
        seg_q, seg_k, seg_v = items

        def per_head(head_index):
            return attend_one(seg_q[:, head_index], seg_k[:, head_index], seg_v[:, head_index])
        return lax.map(per_head, jnp.arange(HEADS))
    row_max, row_sum, weighted = lax.map(per_segment, (picked_q, picked_k, picked_v))
    row_max = jnp.transpose(row_max, (0, 2, 1))
    row_sum = jnp.transpose(row_sum, (0, 2, 1))
    weighted = jnp.transpose(weighted, (0, 2, 1, 3))
    full_max = jnp.where(hits[None, None], row_max[:, :, None, :], NEG_FILL).reshape(-1, HEADS)
    full_sum = jnp.where(hits[None, None], row_sum[:, :, None, :], 0.0).reshape(-1, HEADS)
    full_out = jnp.where(hits[None, None, :, :, None], weighted[:, :, None], 0.0).reshape(-1, HEADS, DH)
    return (full_max, full_sum, full_out)

def merge_levels(running, fresh):
    new_max = jnp.maximum(running[0], fresh[0])
    old_scale = jnp.exp(running[0] - new_max)
    new_scale = jnp.exp(fresh[0] - new_max)
    new_sum = running[1] * old_scale + fresh[1] * new_scale
    new_out = running[2] * old_scale[:, :, None] + fresh[2] * new_scale[:, :, None]
    return (new_max, new_sum, new_out)

def reference(queries, keys, values, offsets, out_weight):
    query_heads = queries.reshape(-1, HEADS, DH)
    key_heads = keys.reshape(-1, HEADS, DH)
    value_heads = values.reshape(-1, HEADS, DH)
    running = level_terms(query_heads, key_heads, value_heads, jnp.zeros((HEADS,), jnp.int32), 1)
    for level_index in range(1, LEVELS):
        fresh = level_terms(query_heads, key_heads, value_heads, offsets[level_index - 1], 2 ** level_index)
        running = merge_levels(running, fresh)
    attended = (running[2] / running[1][:, :, None]).astype(jnp.bfloat16).reshape(-1, HEADS * DH)
    return jnp.dot(attended, out_weight, preferred_element_type=jnp.float32).astype(jnp.bfloat16)
```

```python
import math

import jax
import jax.numpy as jnp
import numpy as np
from jax import lax
from jax.experimental import pallas as pl
from jax.experimental.pallas import tpu as pltpu
from jax.sharding import PartitionSpec as P

DH = 128
LEVELS = 4
CLASSES = 8
HEADS_HERE = 4
TOK = 1536
QUARTER = 384
RUN = QUARTER // CLASSES
SUB = 128
NEG = -1e30
SCALE = math.log2(math.e) / math.sqrt(DH)
MESH = pl.DeviceIdType.MESH
F32 = jnp.float32
BF16 = jnp.bfloat16

QC, KC, VC = 0, TOK, 2 * TOK
N1, N2, N3 = TOK // 2, TOK // 4, TOK // 8
Q1 = 3 * TOK
Q2 = Q1 + N1
Q3 = Q2 + N2
K1 = Q3 + N3
V1 = K1 + N1
K2 = V1 + N1
V2 = K2 + N2
K3 = V2 + N2
V3 = K3 + N3
ROWS = V3 + N3

R0, R1, R2, R3 = 0, TOK, TOK + N1, TOK + N1 + N2
RES = TOK + N1 + N2 + N3


def class_order(tokens):
    return np.arange(tokens).reshape(tokens // CLASSES, CLASSES).T.reshape(-1)


def pick_kernel(off_ref, perm_ref, q_ref, k_ref, v_ref, out_ref):
    head = lax.axis_index("head") * HEADS_HERE + pl.program_id(0)
    perm = perm_ref[...]
    run_sub = SUB // CLASSES
    for source, base in ((q_ref, QC), (k_ref, KC), (v_ref, VC)):
        for sub in range(TOK // SUB):
            moved = jnp.dot(
                perm, source[sub * SUB : (sub + 1) * SUB, :], preferred_element_type=F32
            ).astype(BF16)
            quarter, part = divmod(sub, QUARTER // SUB)
            for c in range(CLASSES):
                row = base + quarter * QUARTER + c * RUN + part * run_sub
                out_ref[0, row : row + run_sub, :] = moved[c * run_sub : (c + 1) * run_sub, :]
    for base, targets in ((QC, (Q1, Q2, Q3)), (KC, (K1, K2, K3)), (VC, (V1, V2, V3))):
        for level in range(1, LEVELS):
            dilation = 2**level
            runs = CLASSES // dilation
            shift = off_ref[level - 1, head]
            for quarter in range(TOK // QUARTER):
                for b in range(runs):
                    row = base + quarter * QUARTER + (dilation * b + shift) * RUN
                    row = pl.multiple_of(row, 16)
                    to = targets[level - 1] + (quarter * runs + b) * RUN
                    out_ref[0, to : to + RUN, :] = out_ref[0, pl.ds(row, RUN), :]


def scores_of(q, k):
    return lax.dot_general(q, k, (((1,), (1,)), ((), ())), preferred_element_type=F32)


def softmax_parts(parts):
    top = None
    for s, _, valid in parts:
        high = jnp.max(s, axis=1, keepdims=True)
        if valid is not None:
            high = jnp.where(valid, high, NEG)
        top = high if top is None else jnp.maximum(top, high)
    weights, values = [], []
    for s, v, valid in parts:
        if valid is None:
            base, one = top, jnp.ones(v.shape, BF16)
        else:
            base = jnp.where(valid, top, 0.0)
            one = jnp.full(v.shape, jnp.where(valid, 1.0, 0.0), F32).astype(BF16)
        weights.append(jnp.exp2((s - base) * SCALE).astype(BF16))
        values.append(jnp.concatenate([v, one], axis=1))
    out = jnp.dot(
        jnp.concatenate(weights, axis=1), jnp.concatenate(values, axis=0), preferred_element_type=F32
    )
    return top, out


def main_kernel(
    off_ref, qkv_hbm, w_hbm, unperm_ref, pq0, pq1, pq2, pk0, pk1, pk2, out_ref,
    qkv, kv1, kv2, kv3, w_vm, abuf, att, ap, res_m, res_l, res_a,
    load_sem, w_sem, r1, r2, r3, ra, s1, s2p, s2y, s2r, s3p, s3y, s3r, sa,
):
    ctx = lax.axis_index("ctx")
    x = lax.axis_index("head")
    core = ctx % 2
    y = (ctx // 2) % 4
    p4 = ctx % 4
    p8 = ctx % 8
    partner = ctx + 1 - 2 * core

    def at_y(step):
        return ctx + 2 * ((y + step) % 4 - y)

    def load(h):
        return pltpu.make_async_copy(qkv_hbm.at[h], qkv.at[h], load_sem.at[h])

    w_copy = pltpu.make_async_copy(w_hbm, w_vm, w_sem)
    for h in range(HEADS_HERE):
        load(h).start()
    w_copy.start()

    barrier = pltpu.get_barrier_semaphore()
    pl.semaphore_signal(barrier, inc=1, device_id={"ctx": partner, "head": x}, device_id_type=MESH)
    for step in range(1, 4):
        pl.semaphore_signal(barrier, inc=1, device_id={"ctx": at_y(step), "head": x}, device_id_type=MESH)
        pl.semaphore_signal(barrier, inc=1, device_id={"ctx": ctx, "head": (x + step) % 4}, device_id_type=MESH)
    pl.semaphore_wait(barrier, 7)

    def remote(source, target, send, recv, to_ctx, to_head):
        return pltpu.make_async_remote_copy(
            src_ref=source, dst_ref=target, send_sem=send, recv_sem=recv,
            device_id={"ctx": to_ctx, "head": to_head}, device_id_type=MESH,
        )

    def send1(h):
        return remote(qkv_hbm.at[h, pl.ds(K1, 2 * N1)], kv1.at[h], s1.at[h], r1.at[h], partner, x)

    def send2_partner(h):
        return remote(qkv_hbm.at[h, pl.ds(K2, 2 * N2)], kv2.at[0, h], s2p.at[h], r2.at[h, 1], partner, x)

    def send2_y(h):
        return remote(qkv_hbm.at[h, pl.ds(K2, 2 * N2)], kv2.at[1, h], s2y.at[h], r2.at[h, 2], at_y(1), x)

    def relay2(h):
        slot = 3 - 2 * core
        return remote(kv2.at[1, h], kv2.at[slot - 1, h], s2r.at[h], r2.at[h, slot], partner, x)

    def send3_partner(h):
        return remote(qkv_hbm.at[h, pl.ds(K3, 2 * N3)], kv3.at[0, h], s3p.at[h], r3.at[h, 1], partner, x)

    def send3_y(h, step):
        return remote(
            qkv_hbm.at[h, pl.ds(K3, 2 * N3)], kv3.at[2 * step - 1, h], s3y.at[h, step],
            r3.at[h, 2 * step], at_y(step), x,
        )

    def relay3(h, step):
        slot = 2 * step + 1 - 2 * core
        return remote(
            kv3.at[2 * step - 1, h], kv3.at[slot - 1, h], s3r.at[h, step], r3.at[h, slot], partner, x
        )

    def send_att(h, step):
        to = (x + step) % 4
        return remote(att.at[h, to], abuf.at[x * HEADS_HERE + h], sa.at[h, step], ra.at[h, step], ctx, to)

    def start_sends(h, carry):
        for step in (3, 2, 1):
            @pl.when(y + step <= 3)
            def _():
                send3_y(h, step).start()
        @pl.when(y % 2 == 0)
        def _():
            send2_y(h).start()
        @pl.when(core == 0)
        def _():
            send1(h).start()
            send2_partner(h).start()
            send3_partner(h).start()
        return carry

    lax.fori_loop(0, HEADS_HERE, start_sends, 0)

    @pl.when(core == 0)
    def _():
        kv1[...] = jnp.zeros(kv1.shape, BF16)
    for slot in range(1, 4):
        @pl.when(slot > p4)
        def _():
            kv2[slot - 1] = jnp.zeros(kv2.shape[1:], BF16)
    for slot in range(1, 8):
        @pl.when(slot > p8)
        def _():
            kv3[slot - 1] = jnp.zeros(kv3.shape[1:], BF16)

    def own(h, row, count):
        return qkv[h, row : row + count, :]

    def keep(row, count, top, out):
        res_m[row : row + count, :] = jnp.broadcast_to(top, (count, DH))
        res_a[row : row + count, :] = out[:, :DH]
        res_l[row : row + count, :] = out[:, DH:]

    def masked(s, pq, pk):
        seen = jnp.concatenate([pq[...]] * (QUARTER // DH), axis=1) >= pk[...]
        return jnp.where(seen, s, NEG)

    def one_head(h, carry):
        pltpu.make_async_copy(qkv_hbm.at[h], qkv.at[h], load_sem.at[h]).wait()
        for i in range(TOK // QUARTER):
            q = own(h, QC + i * QUARTER, QUARTER)
            parts = []
            s = scores_of(q, own(h, KC + i * QUARTER, QUARTER))
            parts.append((masked(s, pq0, pk0), own(h, VC + i * QUARTER, QUARTER), None))
            if i:
                parts.append((scores_of(q, own(h, KC, i * QUARTER)), own(h, VC, i * QUARTER), None))
            top, out = softmax_parts(parts)
            keep(R0 + i * QUARTER, QUARTER, top, out)
        @pl.when(y % 2 == 1)
        def _():
            send2_y(h).wait_recv()
            relay2(h).start()
        for step in (1, 2, 3):
            @pl.when(y >= step)
            def _():
                send3_y(h, step).wait_recv()
                relay3(h, step).start()
        @pl.when(core == 1)
        def _():
            send1(h).wait_recv()
        for i in range(N1 // QUARTER):
            q = own(h, Q1 + i * QUARTER, QUARTER)
            parts = []
            s = scores_of(q, own(h, K1 + i * QUARTER, QUARTER))
            parts.append((masked(s, pq1, pk1), own(h, V1 + i * QUARTER, QUARTER), None))
            if i:
                parts.append((scores_of(q, own(h, K1, i * QUARTER)), own(h, V1, i * QUARTER), None))
            parts.append((scores_of(q, kv1[h, :N1]), kv1[h, N1:], core == 1))
            top, out = softmax_parts(parts)
            keep(R1 + i * QUARTER, QUARTER, top, out)
        for slot in (1, 3):
            @pl.when(slot <= p4)
            def _():
                remote(kv2.at[0, h], kv2.at[slot - 1, h], s2r.at[h], r2.at[h, slot], partner, x).wait_recv()
        q = own(h, Q2, N2)
        parts = [(masked(scores_of(q, own(h, K2, N2)), pq2, pk2), own(h, V2, N2), None)]
        for slot in range(1, 4):
            parts.append((scores_of(q, kv2[slot - 1, h, :N2]), kv2[slot - 1, h, N2:], slot <= p4))
        top, out = softmax_parts(parts)
        keep(R2, N2, top, out)
        for slot in (1, 3, 5, 7):
            @pl.when(slot <= p8)
            def _():
                remote(kv3.at[0, h], kv3.at[slot - 1, h], s3p.at[h], r3.at[h, slot], partner, x).wait_recv()
        q = own(h, Q3, N3)
        keys = jnp.concatenate([own(h, K3, N3)] + [kv3[d, h, :N3] for d in range(7)], axis=0)
        vals = jnp.concatenate([own(h, V3, N3)] + [kv3[d, h, N3:] for d in range(7)], axis=0)
        column = lax.broadcasted_iota(jnp.int32, (1, TOK), 1)
        least = jnp.where(column < N3, column, jnp.where(column < N3 * (p8 + 1), -1, TOK))
        row = lax.broadcasted_iota(jnp.int32, (N3, TOK), 0)
        s = jnp.where(row >= least, scores_of(q, keys), NEG)
        top, out = softmax_parts([(s, vals, None)])
        keep(R3, N3, top, out)
        head = x * HEADS_HERE + h
        shifts = [off_ref[level - 1, head] for level in range(1, LEVELS)]
        for i in range(TOK // QUARTER):
            for c in range(CLASSES):
                rows = [R0 + i * QUARTER + c * RUN]
                picked = [None]
                for level, start in ((1, R1), (2, R2), (3, R3)):
                    dilation = 2**level
                    runs = CLASSES // dilation
                    rows.append(start + (i * runs + c // dilation) * RUN)
                    picked.append(shifts[level - 1] == c % dilation)
                tops = []
                for level in range(LEVELS):
                    m = res_m[rows[level] : rows[level] + RUN, :]
                    tops.append(m if level == 0 else jnp.where(picked[level], m, NEG))
                high = jnp.maximum(jnp.maximum(tops[0], tops[1]), jnp.maximum(tops[2], tops[3]))
                num = den = None
                for level in range(LEVELS):
                    f = jnp.exp2((tops[level] - high) * SCALE)
                    a = f * res_a[rows[level] : rows[level] + RUN, :]
                    l = f * res_l[rows[level] : rows[level] + RUN, :]
                    num = a if num is None else num + a
                    den = l if den is None else den + l
                att[h, i, c * RUN : (c + 1) * RUN, :] = (num / den).astype(BF16)
        for step in (2, 1, 3):
            send_att(h, step).start()
        abuf[x * HEADS_HERE + h] = att[h, x]
        return carry

    lax.fori_loop(0, HEADS_HERE, one_head, 0)

    w_copy.wait()

    def wait_att(h, carry):
        for step in range(1, 4):
            source = (x + 4 - step) % 4
            remote(
                att.at[h, 0], abuf.at[source * HEADS_HERE + h], sa.at[h, step], ra.at[h, step], ctx, (x + step) % 4
            ).wait_recv()
        return carry

    lax.fori_loop(0, HEADS_HERE, wait_att, 0)
    unperm = unperm_ref[...]
    for g in range(4):
        block = jnp.concatenate([abuf[4 * g + i] for i in range(4)], axis=1)
        ap[:, g * 512 : (g + 1) * 512] = jnp.dot(unperm, block, preferred_element_type=F32).astype(BF16)

    def project(n, carry):
        at = pl.multiple_of(n * 256, 256)
        out_ref[:, pl.ds(at, 256)] = jnp.dot(
            ap[...], w_vm[:, pl.ds(at, 256)], preferred_element_type=F32
        ).astype(BF16)
        return carry

    lax.fori_loop(0, 8, project, 0)

    def wait_sends(h, carry):
        for step in (3, 2, 1):
            @pl.when(y + step <= 3)
            def _():
                send3_y(h, step).wait_send()
            @pl.when(y >= step)
            def _():
                relay3(h, step).wait_send()
            send_att(h, step).wait_send()
        @pl.when(y % 2 == 0)
        def _():
            send2_y(h).wait_send()
        @pl.when(y % 2 == 1)
        def _():
            relay2(h).wait_send()
        @pl.when(core == 0)
        def _():
            send1(h).wait_send()
            send2_partner(h).wait_send()
            send3_partner(h).wait_send()
        return carry

    lax.fori_loop(0, HEADS_HERE, wait_sends, 0)


def positions(level):
    row = np.arange(QUARTER)
    if level == 0:
        c, j = row // RUN, row % RUN
        return CLASSES * j + c
    runs = CLASSES // 2**level
    block, b, j = row // (runs * RUN), row // RUN % runs, row % RUN
    return block * runs * RUN + runs * j + b


def body(queries, keys, values, offsets, out_weight):
    order = class_order(SUB)
    perm = jnp.asarray(np.eye(SUB)[order], BF16)
    packed = pl.pallas_call(
        pick_kernel,
        grid=(HEADS_HERE,),
        in_specs=[
            pl.BlockSpec(memory_space=pltpu.SMEM),
            pl.BlockSpec((SUB, SUB), lambda h: (0, 0)),
            pl.BlockSpec((TOK, DH), lambda h: (0, h)),
            pl.BlockSpec((TOK, DH), lambda h: (0, h)),
            pl.BlockSpec((TOK, DH), lambda h: (0, h)),
        ],
        out_specs=pl.BlockSpec((1, ROWS, DH), lambda h: (h, 0, 0)),
        out_shape=jax.ShapeDtypeStruct((HEADS_HERE, ROWS, DH), BF16),
        compiler_params=pltpu.CompilerParams(vmem_limit_bytes=40 * 2**20),
        name="pick",
    )(offsets, perm, queries, keys, values)

    unperm = jnp.asarray(np.eye(QUARTER)[class_order(QUARTER)].T, BF16)
    place = [positions(level) for level in range(3)]
    pq = [jnp.asarray(np.repeat(p[:, None], DH, 1), jnp.int32) for p in place]
    pk = [jnp.asarray(p[None, :], jnp.int32) for p in place]
    vm = pl.BlockSpec(memory_space=pltpu.VMEM)
    hbm = pl.BlockSpec(memory_space=pl.ANY)
    dma = pltpu.SemaphoreType.DMA
    return pl.pallas_call(
        main_kernel,
        in_specs=[pl.BlockSpec(memory_space=pltpu.SMEM), hbm, hbm] + [vm] * 7,
        out_specs=vm,
        out_shape=jax.ShapeDtypeStruct((QUARTER, 2048), BF16),
        scratch_shapes=[
            pltpu.VMEM((HEADS_HERE, ROWS, DH), BF16),
            pltpu.VMEM((HEADS_HERE, 2 * N1, DH), BF16),
            pltpu.VMEM((3, HEADS_HERE, 2 * N2, DH), BF16),
            pltpu.VMEM((7, HEADS_HERE, 2 * N3, DH), BF16),
            pltpu.VMEM((2048, 2048), BF16),
            pltpu.VMEM((16, QUARTER, DH), BF16),
            pltpu.VMEM((HEADS_HERE, 4, QUARTER, DH), BF16),
            pltpu.VMEM((QUARTER, 2048), BF16),
            pltpu.VMEM((RES, DH), F32),
            pltpu.VMEM((RES, DH), F32),
            pltpu.VMEM((RES, DH), F32),
            dma((4,)), dma,
            dma((4,)), dma((4, 4)), dma((4, 8)), dma((4, 4)),
            dma((4,)), dma((4,)), dma((4,)), dma((4,)),
            dma((4,)), dma((4, 4)), dma((4, 4)), dma((4, 4)),
        ],
        compiler_params=pltpu.CompilerParams(
            collective_id=0, has_side_effects=True, vmem_limit_bytes=62 * 2**20
        ),
        name="attend",
    )(offsets, packed, out_weight, unperm, *pq, *pk)


def solution(mesh):
    placed = (P("ctx", "head"), P("ctx", "head"), P("ctx", "head"), P(), P())
    return jax.shard_map(
        body, mesh=mesh, in_specs=placed, out_specs=P(("ctx", "head"), None), check_vma=False
    )
```

```python
import math

import jax
import jax.numpy as jnp
import numpy as np
from jax import lax
from jax.experimental import pallas as pl
from jax.experimental.pallas import tpu as pltpu
from jax.sharding import PartitionSpec as P

DH = 128
LEVELS = 4
CLASSES = 8
HEADS_HERE = 4
TOK = 1536
QUARTER = 384
RUN = QUARTER // CLASSES
SUB = 128
NEG = -1e30
SCALE = math.log2(math.e) / math.sqrt(DH)
MESH = pl.DeviceIdType.MESH
F32 = jnp.float32
BF16 = jnp.bfloat16

QC, KC, VC = 0, TOK, 2 * TOK
N1, N2, N3 = TOK // 2, TOK // 4, TOK // 8
Q1 = 3 * TOK
Q2 = Q1 + N1
Q3 = Q2 + N2
K1 = Q3 + N3
V1 = K1 + N1
K2 = V1 + N1
V2 = K2 + N2
K3 = V2 + N2
V3 = K3 + N3
ROWS = V3 + N3

R2, R3 = 0, N2
RES = N2 + N3


def class_order(tokens):
    return np.arange(tokens).reshape(tokens // CLASSES, CLASSES).T.reshape(-1)


def pick_kernel(off_ref, perm_ref, q_ref, k_ref, v_ref, out_ref):
    head = lax.axis_index("head") * HEADS_HERE + pl.program_id(0)
    perm = perm_ref[...]
    run_sub = SUB // CLASSES
    for source, base in ((q_ref, QC), (k_ref, KC), (v_ref, VC)):
        for sub in range(TOK // SUB):
            moved = jnp.dot(
                perm, source[sub * SUB : (sub + 1) * SUB, :], preferred_element_type=F32
            ).astype(BF16)
            quarter, part = divmod(sub, QUARTER // SUB)
            for c in range(CLASSES):
                row = base + quarter * QUARTER + c * RUN + part * run_sub
                out_ref[0, row : row + run_sub, :] = moved[c * run_sub : (c + 1) * run_sub, :]
    for base, targets in ((QC, (Q1, Q2, Q3)), (KC, (K1, K2, K3)), (VC, (V1, V2, V3))):
        for level in range(1, LEVELS):
            dilation = 2**level
            runs = CLASSES // dilation
            shift = off_ref[level - 1, head]
            for quarter in range(TOK // QUARTER):
                for b in range(runs):
                    row = base + quarter * QUARTER + (dilation * b + shift) * RUN
                    row = pl.multiple_of(row, 16)
                    to = targets[level - 1] + (quarter * runs + b) * RUN
                    out_ref[0, to : to + RUN, :] = out_ref[0, pl.ds(row, RUN), :]


def scores_of(q, k):
    return lax.dot_general(q, k, (((1,), (1,)), ((), ())), preferred_element_type=F32)


def softmax_parts(parts):
    top = None
    for s, _, valid in parts:
        high = jnp.max(s, axis=1, keepdims=True)
        if valid is not None:
            high = jnp.where(valid, high, NEG)
        top = high if top is None else jnp.maximum(top, high)
    weights, values = [], []
    for s, v, valid in parts:
        if valid is None:
            base = top
        else:
            base = jnp.where(valid, top, -NEG)
        weights.append(jnp.exp2((s - base) * SCALE).astype(BF16))
        values.append(jnp.concatenate([v, jnp.ones(v.shape, BF16)], axis=1))
    out = jnp.dot(
        jnp.concatenate(weights, axis=1), jnp.concatenate(values, axis=0), preferred_element_type=F32
    )
    return top, out


def pipelined(tiles):
    parts = tiles[0][0]()
    for at, (_, finish) in enumerate(tiles):
        ahead = tiles[at + 1][0]() if at + 1 < len(tiles) else None
        finish(*softmax_parts(parts))
        parts = ahead


def main_kernel(
    off_ref, qkv_hbm, w_hbm, unperm_ref, pq0, pq1, pq2, pk0, pk1, pk2, out_ref,
    qkv, kv1, kv2, kv3, passing, qfar, farout, farstat, gota, gots, w_vm, abuf, att, ap, total, res0, res1, res_m, res_l, res_a,
    load_sem, w_sem, r1, r2, rq, rfa, rfs, r3, rp, ra, s1, s2p, sq, sfa, sfs, s3p, s3y, s3r, s3f, sa,
):
    ctx = lax.axis_index("ctx")
    x = lax.axis_index("head")
    core = ctx % 2
    y = (ctx // 2) % 4
    p8 = ctx % 8
    partner = ctx + 1 - 2 * core

    def at_y(step):
        return ctx + 2 * ((y + step) % 4 - y)

    def load(h):
        return pltpu.make_async_copy(qkv_hbm.at[h], qkv.at[h], load_sem.at[h])

    w_copy = pltpu.make_async_copy(w_hbm, w_vm, w_sem)
    for h in range(HEADS_HERE):
        load(h).start()

    barrier = pltpu.get_barrier_semaphore()
    pl.semaphore_signal(barrier, inc=1, device_id={"ctx": partner, "head": x}, device_id_type=MESH)
    for step in range(1, 4):
        pl.semaphore_signal(barrier, inc=1, device_id={"ctx": at_y(step), "head": x}, device_id_type=MESH)
        pl.semaphore_signal(barrier, inc=1, device_id={"ctx": ctx, "head": (x + step) % 4}, device_id_type=MESH)
    pl.semaphore_wait(barrier, 7)

    def remote(source, target, send, recv, to_ctx, to_head):
        return pltpu.make_async_remote_copy(
            src_ref=source, dst_ref=target, send_sem=send, recv_sem=recv,
            device_id={"ctx": to_ctx, "head": to_head}, device_id_type=MESH,
        )

    def send1(h):
        return remote(qkv_hbm.at[h, pl.ds(K1, 2 * N1)], kv1.at[h], s1.at[h], r1.at[h], partner, x)

    def send2_partner(h):
        return remote(qkv_hbm.at[h, pl.ds(K2, 2 * N2)], kv2.at[h], s2p.at[h], r2.at[h], partner, x)

    def send_q(h):
        return remote(qkv_hbm.at[h, pl.ds(Q2, N2)], qfar.at[h], sq.at[h], rq.at[h], at_y(3), x)

    def send_far(h):
        return remote(farout.at[h], gota.at[h], sfa.at[h], rfa.at[h], at_y(1), x)

    def send_stat(h):
        return remote(farstat.at[h], gots.at[h], sfs.at[h], rfs.at[h], at_y(1), x)

    def send3_partner(h):
        return remote(qkv_hbm.at[h, pl.ds(K3, 2 * N3)], kv3.at[0, h], s3p.at[h], r3.at[h, 1], partner, x)

    def send3_y(h, step):
        return remote(
            qkv_hbm.at[h, pl.ds(K3, 2 * N3)], kv3.at[2 * step - 1, h], s3y.at[h, step],
            r3.at[h, 2 * step], at_y(step), x,
        )

    def send3_via(h):
        return remote(qkv_hbm.at[h, pl.ds(K3, 2 * N3)], passing.at[h], s3y.at[h, 2], rp.at[h], at_y(3), x)

    def forward3_up(h):
        return remote(passing.at[h], kv3.at[3, h], s3f.at[h], r3.at[h, 4], at_y(3), x)

    def forward3_down(h):
        return remote(kv3.at[5, h], kv3.at[3, h], s3f.at[h], r3.at[h, 4], at_y(3), x)

    def relay3(h, step):
        slot = 2 * step + 1 - 2 * core
        return remote(
            kv3.at[2 * step - 1, h], kv3.at[slot - 1, h], s3r.at[h, step], r3.at[h, slot], partner, x
        )

    def send_att(h, step):
        to = (x + step) % 4
        return remote(att.at[h, to], abuf.at[x * HEADS_HERE + h], sa.at[h, step], ra.at[h, step], ctx, to)

    def start_sends(h, carry):
        @pl.when(y % 2 == 1)
        def _():
            send_q(h).start()
        @pl.when(y == 0)
        def _():
            send3_y(h, 3).start()
        @pl.when(y == 1)
        def _():
            send3_via(h).start()
        @pl.when(y <= 2)
        def _():
            send3_y(h, 1).start()
        send2_partner(h).start()
        @pl.when(core == 0)
        def _():
            send1(h).start()
            send3_partner(h).start()
        return carry

    lax.fori_loop(0, HEADS_HERE, start_sends, 0)

    def clear():
        @pl.when(core == 0)
        def _():
            kv1[...] = jnp.zeros(kv1.shape, BF16)
        for slot in range(1, 8):
            @pl.when(slot > p8)
            def _():
                kv3[slot - 1] = jnp.zeros(kv3.shape[1:], BF16)

    def own(h, row, count):
        return qkv[h, row : row + count, :]

    def keep(row, count, top, out):
        res_m[row : row + count, :] = jnp.broadcast_to(top, (count, DH))
        res_a[row : row + count, :] = out[:, :DH]
        res_l[row : row + count, :] = out[:, DH:]

    def masked(s, pq, pk):
        seen = jnp.concatenate([pq[...]] * (QUARTER // DH), axis=1) >= pk[...]
        return jnp.where(seen, s, NEG)

    def level0(h):
        pltpu.make_async_copy(qkv_hbm.at[h], qkv.at[h], load_sem.at[h]).wait()
        def tile(i):
            def scores():
                q = own(h, QC + i * QUARTER, QUARTER)
                near = masked(scores_of(q, own(h, KC + i * QUARTER, QUARTER)), pq0, pk0)
                parts = [(near, own(h, VC + i * QUARTER, QUARTER), None)]
                if i:
                    parts.append((scores_of(q, own(h, KC, i * QUARTER)), own(h, VC, i * QUARTER), None))
                return parts

            def finish(top, out):
                rows = slice(i * QUARTER, (i + 1) * QUARTER)
                res0[h % 3, 0, rows, :] = jnp.broadcast_to(top, (QUARTER, DH))
                res0[h % 3, 1, rows, :] = out[:, :DH]
                res0[h % 3, 2, rows, :] = out[:, DH:]

            return scores, finish

        pipelined([tile(i) for i in (3, 2, 1, 0)])

    def pass_far(h):
        @pl.when(y == 0)
        def _():
            send3_via(h).wait_recv()
            forward3_up(h).start()
        @pl.when(y == 3)
        def _():
            send3_y(h, 3).wait_recv()
            forward3_down(h).start()
            relay3(h, 3).start()

    def pass_near(h):
        for step in (1, 2):
            @pl.when(y >= step)
            def _():
                send3_y(h, step).wait_recv()
                relay3(h, step).start()

    def level1(h):
        @pl.when(core == 1)
        def _():
            send1(h).wait_recv()
        def tile(i):
            def scores():
                q = own(h, Q1 + i * QUARTER, QUARTER)
                near = masked(scores_of(q, own(h, K1 + i * QUARTER, QUARTER)), pq1, pk1)
                parts = [(near, own(h, V1 + i * QUARTER, QUARTER), None)]
                if i:
                    parts.append((scores_of(q, own(h, K1, i * QUARTER)), own(h, V1, i * QUARTER), None))
                parts.append((scores_of(q, kv1[h, :N1]), kv1[h, N1:], core == 1))
                return parts

            def finish(top, out):
                rows = slice(i * QUARTER, (i + 1) * QUARTER)
                res1[h % 2, 0, rows, :] = jnp.broadcast_to(top, (QUARTER, DH))
                res1[h % 2, 1, rows, :] = out[:, :DH]
                res1[h % 2, 2, rows, :] = out[:, DH:]

            return scores, finish

        pipelined([tile(1), tile(0)])

    def far(h):
        send_q(h).wait_recv()
        q = qfar[h]
        top, out = softmax_parts([
            (scores_of(q, own(h, K2, N2)), own(h, V2, N2), None),
            (scores_of(q, kv2[h, :N2]), kv2[h, N2:], None),
        ])
        farout[h] = out[:, :DH].astype(BF16)
        lane = lax.broadcasted_iota(jnp.int32, (N2, DH), 1)
        both = jnp.where(lane < DH // 2, jnp.broadcast_to(top, (N2, DH)), out[:, DH:]).T
        farstat[h, :8, :] = both[:8, :]
        farstat[h, 8:, :] = both[DH // 2 : DH // 2 + 8, :]
        send_far(h).start()
        send_stat(h).start()

    def join_far(h):
        send_far(h).wait_recv()
        send_stat(h).wait_recv()
        m_far = jnp.broadcast_to(gots[h, 0:1, :], (DH, N2)).T
        l_far = jnp.broadcast_to(gots[h, 8:9, :], (DH, N2)).T
        rows = slice(R2, R2 + N2)
        m = res_m[rows, :]
        high = jnp.maximum(m, m_far)
        here = jnp.exp2((m - high) * SCALE)
        there = jnp.exp2((m_far - high) * SCALE)
        res_m[rows, :] = high
        res_l[rows, :] = here * res_l[rows, :] + there * l_far
        res_a[rows, :] = here * res_a[rows, :] + there * gota[h].astype(F32)

    def rest(h):
        for slot in (1, 3, 5, 7):
            @pl.when(slot <= p8)
            def _():
                remote(kv3.at[0, h], kv3.at[slot - 1, h], s3p.at[h], r3.at[h, slot], partner, x).wait_recv()
        def scores2():
            q = own(h, Q2, N2)
            parts = [(masked(scores_of(q, own(h, K2, N2)), pq2, pk2), own(h, V2, N2), None)]
            parts.append((scores_of(q, kv2[h, :N2]), kv2[h, N2:], core == 1))
            return parts

        def scores3():
            keys = jnp.concatenate([own(h, K3, N3)] + [kv3[d, h, :N3] for d in range(7)], axis=0)
            vals = jnp.concatenate([own(h, V3, N3)] + [kv3[d, h, N3:] for d in range(7)], axis=0)
            column = lax.broadcasted_iota(jnp.int32, (1, TOK), 1)
            least = jnp.where(column < N3, column, jnp.where(column < N3 * (p8 + 1), -1, TOK))
            row = lax.broadcasted_iota(jnp.int32, (N3, TOK), 0)
            return [(jnp.where(row >= least, scores_of(own(h, Q3, N3), keys), NEG), vals, None)]

        head = x * HEADS_HERE + h
        shifts = [off_ref[level - 1, head] for level in range(1, LEVELS)]

        def joined(terms):
            high = terms[0][0]
            for m, _, _ in terms[1:]:
                high = jnp.maximum(high, m)
            num = den = None
            for m, a, l in terms:
                f = jnp.exp2((m - high) * SCALE)
                num = f * a if num is None else num + f * a
                den = f * l if den is None else den + f * l
            return high, num, den

        def base_term(i, c):
            rows = slice(i * QUARTER + c * RUN, i * QUARTER + c * RUN + RUN)
            return [res0[h % 3, part, rows, :] for part in range(3)]

        def level_term(level, start, i, c):
            dilation = 2**level
            at = start + (i * (CLASSES // dilation) + c // dilation) * RUN
            rows = slice(at, at + RUN)
            if level == 1:
                m, a, l = (res1[h % 2, part, rows, :] for part in range(3))
            else:
                m, a, l = res_m[rows, :], res_a[rows, :], res_l[rows, :]
            return jnp.where(shifts[level - 1] == c % dilation, m, NEG), a, l

        parts2 = scores2()
        parts3 = scores3()
        keep(R2, N2, *softmax_parts(parts2))
        keep(R3, N3, *softmax_parts(parts3))
        @pl.when(y % 2 == 1)
        def _():
            join_far(h)
        for i in range(TOK // QUARTER):
            for c in range(CLASSES):
                terms = [base_term(i, c)]
                for level, start in ((1, 0), (2, R2), (3, R3)):
                    terms.append(level_term(level, start, i, c))
                _, num, den = joined(terms)
                att[h, i, c * RUN : (c + 1) * RUN, :] = (num / den).astype(BF16)
        for step in (2, 1, 3):
            send_att(h, step).start()
        abuf[x * HEADS_HERE + h] = att[h, x]

    def one_step(step, carry):
        h = step - 1
        @pl.when(step < HEADS_HERE)
        def _():
            level0(step)
        @pl.when(step == 2)
        def _():
            w_copy.start()
        @pl.when(step >= 2)
        def _():
            pass_near(h - 1)
        @pl.when((h >= 0) & (h < HEADS_HERE))
        def _():
            level1(h)
            pass_far(h)
            send2_partner(h).wait_recv()
            @pl.when(y % 2 == 0)
            def _():
                far(h)
        @pl.when(step == 0)
        def _():
            clear()
        @pl.when(step >= 2)
        def _():
            rest(h - 1)
        return carry

    lax.fori_loop(0, HEADS_HERE + 2, one_step, 0)

    w_copy.wait()

    def wait_att(h, carry):
        for step in range(1, 4):
            source = (x + 4 - step) % 4
            remote(
                att.at[h, 0], abuf.at[source * HEADS_HERE + h], sa.at[h, step], ra.at[h, step], ctx, (x + step) % 4
            ).wait_recv()
        return carry

    unperm = unperm_ref[...]
    lax.fori_loop(0, HEADS_HERE - 1, wait_att, 0)
    for g in range(4):
        block = jnp.concatenate([abuf[4 * g + i] for i in range(3)], axis=1)
        ap[:, g * 384 : (g + 1) * 384] = jnp.dot(unperm, block, preferred_element_type=F32).astype(BF16)

    def project_first(n, carry):
        at = pl.multiple_of(n * 256, 256)
        weight = jnp.concatenate([w_vm[g * 512 : g * 512 + 384, pl.ds(at, 256)] for g in range(4)], axis=0)
        total[:, pl.ds(at, 256)] = jnp.dot(ap[:, :1536], weight, preferred_element_type=F32)
        return carry

    lax.fori_loop(0, 8, project_first, 0)
    wait_att(HEADS_HERE - 1, 0)
    block = jnp.concatenate([abuf[4 * g + 3] for g in range(4)], axis=1)
    ap[:, 1536:] = jnp.dot(unperm, block, preferred_element_type=F32).astype(BF16)

    def project_last(n, carry):
        at = pl.multiple_of(n * 256, 256)
        weight = jnp.concatenate([w_vm[g * 512 + 384 : g * 512 + 512, pl.ds(at, 256)] for g in range(4)], axis=0)
        out_ref[:, pl.ds(at, 256)] = (
            total[:, pl.ds(at, 256)] + jnp.dot(ap[:, 1536:], weight, preferred_element_type=F32)
        ).astype(BF16)
        return carry

    lax.fori_loop(0, 8, project_last, 0)

    def wait_sends(h, carry):
        @pl.when(y == 0)
        def _():
            send3_y(h, 3).wait_send()
            forward3_up(h).wait_send()
        @pl.when(y == 1)
        def _():
            send3_via(h).wait_send()
        @pl.when(y == 3)
        def _():
            forward3_down(h).wait_send()
        @pl.when(y <= 2)
        def _():
            send3_y(h, 1).wait_send()
        for step in (1, 2, 3):
            @pl.when(y >= step)
            def _():
                relay3(h, step).wait_send()
            send_att(h, step).wait_send()
        @pl.when(y % 2 == 0)
        def _():
            send_far(h).wait_send()
            send_stat(h).wait_send()
        @pl.when(y % 2 == 1)
        def _():
            send_q(h).wait_send()
        send2_partner(h).wait_send()
        @pl.when(core == 0)
        def _():
            send1(h).wait_send()
            send3_partner(h).wait_send()
        return carry

    lax.fori_loop(0, HEADS_HERE, wait_sends, 0)


def positions(level):
    row = np.arange(QUARTER)
    if level == 0:
        c, j = row // RUN, row % RUN
        return CLASSES * j + c
    runs = CLASSES // 2**level
    block, b, j = row // (runs * RUN), row // RUN % runs, row % RUN
    return block * runs * RUN + runs * j + b


def body(queries, keys, values, offsets, out_weight):
    order = class_order(SUB)
    perm = jnp.asarray(np.eye(SUB)[order], BF16)
    packed = pl.pallas_call(
        pick_kernel,
        grid=(HEADS_HERE,),
        in_specs=[
            pl.BlockSpec(memory_space=pltpu.SMEM),
            pl.BlockSpec((SUB, SUB), lambda h: (0, 0)),
            pl.BlockSpec((TOK, DH), lambda h: (0, h)),
            pl.BlockSpec((TOK, DH), lambda h: (0, h)),
            pl.BlockSpec((TOK, DH), lambda h: (0, h)),
        ],
        out_specs=pl.BlockSpec((1, ROWS, DH), lambda h: (h, 0, 0)),
        out_shape=jax.ShapeDtypeStruct((HEADS_HERE, ROWS, DH), BF16),
        compiler_params=pltpu.CompilerParams(vmem_limit_bytes=63 * 2**20),
        name="pick",
    )(offsets, perm, queries, keys, values)

    unperm = jnp.asarray(np.eye(QUARTER)[class_order(QUARTER)].T, BF16)
    place = [positions(level) for level in range(3)]
    pq = [jnp.asarray(np.repeat(p[:, None], DH, 1), jnp.int32) for p in place]
    pk = [jnp.asarray(p[None, :], jnp.int32) for p in place]
    vm = pl.BlockSpec(memory_space=pltpu.VMEM)
    hbm = pl.BlockSpec(memory_space=pl.ANY)
    dma = pltpu.SemaphoreType.DMA
    return pl.pallas_call(
        main_kernel,
        in_specs=[pl.BlockSpec(memory_space=pltpu.SMEM), hbm, hbm] + [vm] * 7,
        out_specs=vm,
        out_shape=jax.ShapeDtypeStruct((QUARTER, 2048), BF16),
        scratch_shapes=[
            pltpu.VMEM((HEADS_HERE, ROWS, DH), BF16),
            pltpu.VMEM((HEADS_HERE, 2 * N1, DH), BF16),
            pltpu.VMEM((HEADS_HERE, 2 * N2, DH), BF16),
            pltpu.VMEM((7, HEADS_HERE, 2 * N3, DH), BF16),
            pltpu.VMEM((HEADS_HERE, 2 * N3, DH), BF16),
            pltpu.VMEM((HEADS_HERE, N2, DH), BF16),
            pltpu.VMEM((HEADS_HERE, N2, DH), BF16),
            pltpu.VMEM((HEADS_HERE, 16, N2), F32),
            pltpu.VMEM((HEADS_HERE, N2, DH), BF16),
            pltpu.VMEM((HEADS_HERE, 16, N2), F32),
            pltpu.VMEM((2048, 2048), BF16),
            pltpu.VMEM((16, QUARTER, DH), BF16),
            pltpu.VMEM((HEADS_HERE, 4, QUARTER, DH), BF16),
            pltpu.VMEM((QUARTER, 2048), BF16),
            pltpu.VMEM((QUARTER, 2048), F32),
            pltpu.VMEM((3, 3, TOK, DH), F32),
            pltpu.VMEM((2, 3, N1, DH), F32),
            pltpu.VMEM((RES, DH), F32),
            pltpu.VMEM((RES, DH), F32),
            pltpu.VMEM((RES, DH), F32),
            dma((4,)), dma,
            dma((4,)), dma((4,)), dma((4,)), dma((4,)), dma((4,)), dma((4, 8)), dma((4,)), dma((4, 4)),
            dma((4,)), dma((4,)), dma((4,)), dma((4,)), dma((4,)),
            dma((4,)), dma((4, 4)), dma((4, 4)), dma((4,)), dma((4, 4)),
        ],
        compiler_params=pltpu.CompilerParams(
            collective_id=0, has_side_effects=True, vmem_limit_bytes=62 * 2**20
        ),
        name="attend",
    )(offsets, packed, out_weight, unperm, *pq, *pk)


def solution(mesh):
    placed = (P("ctx", "head"), P("ctx", "head"), P("ctx", "head"), P(), P())
    return jax.shard_map(
        body, mesh=mesh, in_specs=placed, out_specs=P(("ctx", "head"), None), check_vma=False
    )
```

```python
import math

import jax
import jax.numpy as jnp
import numpy as np
from jax import lax
from jax.experimental import pallas as pl
from jax.experimental.pallas import tpu as pltpu
from jax.sharding import PartitionSpec as P

DH = 128
LEVELS = 4
CLASSES = 8
HEADS_HERE = 4
TOK = 1536
QUARTER = 384
RUN = QUARTER // CLASSES
SUB = 128
NEG = -1e30
SCALE = math.log2(math.e) / math.sqrt(DH)
MESH = pl.DeviceIdType.MESH
F32 = jnp.float32
BF16 = jnp.bfloat16

QC, KC, VC = 0, TOK, 2 * TOK
N1, N2, N3 = TOK // 2, TOK // 4, TOK // 8
Q1 = 3 * TOK
Q2 = Q1 + N1
Q3 = Q2 + N2
K1 = Q3 + N3
V1 = K1 + N1
K2 = V1 + N1
V2 = K2 + N2
K3 = V2 + N2
V3 = K3 + N3
ROWS = V3 + N3

R2, R3 = 0, N2
RES = N2 + N3


def class_order(tokens):
    return np.arange(tokens).reshape(tokens // CLASSES, CLASSES).T.reshape(-1)


def scores_of(q, k):
    return lax.dot_general(q, k, (((1,), (1,)), ((), ())), preferred_element_type=F32)


def softmax_parts(parts):
    top = None
    for s, _, valid in parts:
        high = jnp.max(s, axis=1, keepdims=True)
        if valid is not None:
            high = jnp.where(valid, high, NEG)
        top = high if top is None else jnp.maximum(top, high)
    weights, values = [], []
    for s, v, valid in parts:
        if valid is None:
            base = top
        else:
            base = jnp.where(valid, top, -NEG)
        weights.append(jnp.exp2((s - base) * SCALE).astype(BF16))
        values.append(jnp.concatenate([v, jnp.ones(v.shape, BF16)], axis=1))
    out = jnp.dot(
        jnp.concatenate(weights, axis=1), jnp.concatenate(values, axis=0), preferred_element_type=F32
    )
    return top, out


def pipelined(tiles):
    parts = tiles[0][0]()
    for at, (_, finish) in enumerate(tiles):
        ahead = tiles[at + 1][0]() if at + 1 < len(tiles) else None
        finish(*softmax_parts(parts))
        parts = ahead


def main_kernel(
    off_ref, q_hbm, k_hbm, v_hbm, w_hbm, perm_ref, unperm_ref, pq0, pq1, pq2, pk0, pk1, pk2, out_ref,
    raw, qkv, kv1, kv2, kv3, passing, qfar, farout, farstat, gota, gots, w_vm, abuf, att, ap, total, res0, res1, res_m, res_l, res_a,
    load_sem, w_sem, r1, r2, rq, rfa, rfs, r3, rp, ra, s1, s2p, sq, sfa, sfs, s3p, s3y, s3r, s3f, sa,
):
    ctx = lax.axis_index("ctx")
    x = lax.axis_index("head")
    core = ctx % 2
    y = (ctx // 2) % 4
    p8 = ctx % 8
    partner = ctx + 1 - 2 * core

    def at_y(step):
        return ctx + 2 * ((y + step) % 4 - y)

    def load(h, which):
        source = (q_hbm, k_hbm, v_hbm)[which]
        return pltpu.make_async_copy(
            source.at[:, pl.ds(h * DH, DH)], raw.at[h, which], load_sem.at[h, which]
        )

    w_copy = pltpu.make_async_copy(w_hbm, w_vm, w_sem)
    for h in range(HEADS_HERE):
        for which in range(3):
            load(h, which).start()

    barrier = pltpu.get_barrier_semaphore()
    pl.semaphore_signal(barrier, inc=1, device_id={"ctx": partner, "head": x}, device_id_type=MESH)
    for step in range(1, 4):
        pl.semaphore_signal(barrier, inc=1, device_id={"ctx": at_y(step), "head": x}, device_id_type=MESH)
        pl.semaphore_signal(barrier, inc=1, device_id={"ctx": ctx, "head": (x + step) % 4}, device_id_type=MESH)
    pl.semaphore_wait(barrier, 7)

    def remote(source, target, send, recv, to_ctx, to_head):
        return pltpu.make_async_remote_copy(
            src_ref=source, dst_ref=target, send_sem=send, recv_sem=recv,
            device_id={"ctx": to_ctx, "head": to_head}, device_id_type=MESH,
        )

    def send1(h):
        return remote(qkv.at[h, pl.ds(K1, 2 * N1)], kv1.at[h], s1.at[h], r1.at[h], partner, x)

    def send2_partner(h):
        return remote(qkv.at[h, pl.ds(K2, 2 * N2)], kv2.at[h], s2p.at[h], r2.at[h], partner, x)

    def send_q(h):
        return remote(qkv.at[h, pl.ds(Q2, N2)], qfar.at[h], sq.at[h], rq.at[h], at_y(3), x)

    def send_far(h):
        return remote(farout.at[h], gota.at[h], sfa.at[h], rfa.at[h], at_y(1), x)

    def send_stat(h):
        return remote(farstat.at[h], gots.at[h], sfs.at[h], rfs.at[h], at_y(1), x)

    def send3_partner(h):
        return remote(qkv.at[h, pl.ds(K3, 2 * N3)], kv3.at[0, h], s3p.at[h], r3.at[h, 1], partner, x)

    def send3_y(h, step):
        return remote(
            qkv.at[h, pl.ds(K3, 2 * N3)], kv3.at[2 * step - 1, h], s3y.at[h, step],
            r3.at[h, 2 * step], at_y(step), x,
        )

    def send3_via(h):
        return remote(qkv.at[h, pl.ds(K3, 2 * N3)], passing.at[h], s3y.at[h, 2], rp.at[h], at_y(3), x)

    def forward3_up(h):
        return remote(passing.at[h], kv3.at[3, h], s3f.at[h], r3.at[h, 4], at_y(3), x)

    def forward3_down(h):
        return remote(kv3.at[5, h], kv3.at[3, h], s3f.at[h], r3.at[h, 4], at_y(3), x)

    def relay3(h, step):
        slot = 2 * step + 1 - 2 * core
        return remote(
            kv3.at[2 * step - 1, h], kv3.at[slot - 1, h], s3r.at[h, step], r3.at[h, slot], partner, x
        )

    def send_att(h, step):
        to = (x + step) % 4
        return remote(att.at[h, to], abuf.at[x * HEADS_HERE + h], sa.at[h, step], ra.at[h, step], ctx, to)

    def start_sends(h, carry):
        @pl.when(y % 2 == 1)
        def _():
            send_q(h).start()
        @pl.when(y == 0)
        def _():
            send3_y(h, 3).start()
        @pl.when(y == 1)
        def _():
            send3_via(h).start()
        @pl.when(y <= 2)
        def _():
            send3_y(h, 1).start()
        send2_partner(h).start()
        @pl.when(core == 0)
        def _():
            send1(h).start()
            send3_partner(h).start()
        return carry

    def pick(h, carry):
        head = x * HEADS_HERE + h
        perm = perm_ref[...]
        run_sub = SUB // CLASSES
        for which in range(3):
            pltpu.make_async_copy(q_hbm.at[:, pl.ds(0, DH)], raw.at[h, which], load_sem.at[h, which]).wait()
        pieces = [(which, base, sub) for sub in range(TOK // SUB) for which, base in enumerate((QC, KC, VC))]
        for first in range(0, len(pieces), 6):
            group = pieces[first : first + 6]
            block = jnp.concatenate(
                [raw[h, which, sub * SUB : (sub + 1) * SUB, :] for which, _, sub in group], axis=1
            )
            moved = jnp.dot(perm, block, preferred_element_type=F32).astype(BF16)
            for at, (_, base, sub) in enumerate(group):
                quarter, part = divmod(sub, QUARTER // SUB)
                for c in range(CLASSES):
                    row = base + quarter * QUARTER + c * RUN + part * run_sub
                    qkv[h, row : row + run_sub, :] = moved[
                        c * run_sub : (c + 1) * run_sub, at * DH : (at + 1) * DH
                    ]
        for base, targets in ((QC, (Q1, Q2, Q3)), (KC, (K1, K2, K3)), (VC, (V1, V2, V3))):
            for level in range(1, LEVELS):
                dilation = 2**level
                runs = CLASSES // dilation
                shift = off_ref[level - 1, head]
                for quarter in range(TOK // QUARTER):
                    for b in range(runs):
                        row = base + quarter * QUARTER + dilation * b * RUN
                        to = targets[level - 1] + (quarter * runs + b) * RUN
                        found = qkv[h, row : row + RUN, :]
                        for c in range(1, dilation):
                            other = qkv[h, row + c * RUN : row + c * RUN + RUN, :]
                            found = jnp.where(shift == c, other, found)
                        qkv[h, to : to + RUN, :] = found
        @pl.when(h > 0)
        def _():
            start_sends(h - 1, 0)
        return carry

    lax.fori_loop(0, HEADS_HERE, pick, 0)
    start_sends(HEADS_HERE - 1, 0)

    def clear():
        @pl.when(core == 0)
        def _():
            kv1[...] = jnp.zeros(kv1.shape, BF16)
        for slot in range(1, 8):
            @pl.when((slot > p8) & ((y > 0) | (slot == 1)))
            def _():
                kv3[slot - 1] = jnp.zeros(kv3.shape[1:], BF16)

    def own(h, row, count):
        return qkv[h, row : row + count, :]

    def keep(row, count, top, out):
        res_m[row : row + count, :] = jnp.broadcast_to(top, (count, DH))
        res_a[row : row + count, :] = out[:, :DH]
        res_l[row : row + count, :] = out[:, DH:]

    def masked(s, pq, pk):
        seen = jnp.concatenate([pq[...]] * (QUARTER // DH), axis=1) >= pk[...]
        return jnp.where(seen, s, NEG)

    def level0(h):
        def tile(i):
            def scores():
                q = own(h, QC + i * QUARTER, QUARTER)
                near = masked(scores_of(q, own(h, KC + i * QUARTER, QUARTER)), pq0, pk0)
                parts = [(near, own(h, VC + i * QUARTER, QUARTER), None)]
                if i:
                    parts.append((scores_of(q, own(h, KC, i * QUARTER)), own(h, VC, i * QUARTER), None))
                return parts

            def finish(top, out):
                rows = slice(i * QUARTER, (i + 1) * QUARTER)
                res0[h % 3, 0, rows, :] = jnp.broadcast_to(top, (QUARTER, DH))
                res0[h % 3, 1, rows, :] = out[:, :DH]
                res0[h % 3, 2, rows, :] = out[:, DH:]

            return scores, finish

        pipelined([tile(i) for i in (3, 2, 1, 0)])

    def pass_far(h):
        @pl.when(y == 0)
        def _():
            send3_via(h).wait_recv()
            forward3_up(h).start()
        @pl.when(y == 3)
        def _():
            send3_y(h, 3).wait_recv()
            forward3_down(h).start()
            relay3(h, 3).start()

    def pass_near(h):
        for step in (1, 2):
            @pl.when(y >= step)
            def _():
                send3_y(h, step).wait_recv()
                relay3(h, step).start()

    def level1(h):
        @pl.when(core == 1)
        def _():
            send1(h).wait_recv()
        def tile(i):
            def scores():
                q = own(h, Q1 + i * QUARTER, QUARTER)
                near = masked(scores_of(q, own(h, K1 + i * QUARTER, QUARTER)), pq1, pk1)
                parts = [(near, own(h, V1 + i * QUARTER, QUARTER), None)]
                if i:
                    parts.append((scores_of(q, own(h, K1, i * QUARTER)), own(h, V1, i * QUARTER), None))
                parts.append((scores_of(q, kv1[h, :N1]), kv1[h, N1:], core == 1))
                return parts

            def finish(top, out):
                rows = slice(i * QUARTER, (i + 1) * QUARTER)
                res1[h % 2, 0, rows, :] = jnp.broadcast_to(top, (QUARTER, DH))
                res1[h % 2, 1, rows, :] = out[:, :DH]
                res1[h % 2, 2, rows, :] = out[:, DH:]

            return scores, finish

        pipelined([tile(1), tile(0)])

    def far(h):
        send_q(h).wait_recv()
        q = qfar[h]
        top, out = softmax_parts([
            (scores_of(q, own(h, K2, N2)), own(h, V2, N2), None),
            (scores_of(q, kv2[h, :N2]), kv2[h, N2:], None),
        ])
        farout[h] = out[:, :DH].astype(BF16)
        lane = lax.broadcasted_iota(jnp.int32, (N2, DH), 1)
        both = jnp.where(lane < DH // 2, jnp.broadcast_to(top, (N2, DH)), out[:, DH:]).T
        farstat[h, :8, :] = both[:8, :]
        farstat[h, 8:, :] = both[DH // 2 : DH // 2 + 8, :]
        send_far(h).start()
        send_stat(h).start()

    def join_far(h):
        send_far(h).wait_recv()
        send_stat(h).wait_recv()
        m_far = jnp.broadcast_to(gots[h, 0:1, :], (DH, N2)).T
        l_far = jnp.broadcast_to(gots[h, 8:9, :], (DH, N2)).T
        rows = slice(R2, R2 + N2)
        m = res_m[rows, :]
        high = jnp.maximum(m, m_far)
        here = jnp.exp2((m - high) * SCALE)
        there = jnp.exp2((m_far - high) * SCALE)
        res_m[rows, :] = high
        res_l[rows, :] = here * res_l[rows, :] + there * l_far
        res_a[rows, :] = here * res_a[rows, :] + there * gota[h].astype(F32)

    def rest(h):
        for slot in (1, 3, 5, 7):
            @pl.when(slot <= p8)
            def _():
                remote(kv3.at[0, h], kv3.at[slot - 1, h], s3p.at[h], r3.at[h, slot], partner, x).wait_recv()
        def scores2():
            q = own(h, Q2, N2)
            parts = [(masked(scores_of(q, own(h, K2, N2)), pq2, pk2), own(h, V2, N2), None)]
            parts.append((scores_of(q, kv2[h, :N2]), kv2[h, N2:], core == 1))
            return parts

        def scores3(slots):
            width = (slots + 1) * N3
            keys = jnp.concatenate([own(h, K3, N3)] + [kv3[d, h, :N3] for d in range(slots)], axis=0)
            vals = jnp.concatenate([own(h, V3, N3)] + [kv3[d, h, N3:] for d in range(slots)], axis=0)
            column = lax.broadcasted_iota(jnp.int32, (1, width), 1)
            least = jnp.where(column < N3, column, jnp.where(column < N3 * (p8 + 1), -1, TOK))
            row = lax.broadcasted_iota(jnp.int32, (N3, width), 0)
            return [(jnp.where(row >= least, scores_of(own(h, Q3, N3), keys), NEG), vals, None)]

        head = x * HEADS_HERE + h
        shifts = [off_ref[level - 1, head] for level in range(1, LEVELS)]

        def joined(terms):
            high = terms[0][0]
            for m, _, _ in terms[1:]:
                high = jnp.maximum(high, m)
            num = den = None
            for m, a, l in terms:
                f = jnp.exp2((m - high) * SCALE)
                num = f * a if num is None else num + f * a
                den = f * l if den is None else den + f * l
            return high, num, den

        def base_term(i, c):
            rows = slice(i * QUARTER + c * RUN, i * QUARTER + c * RUN + RUN)
            return [res0[h % 3, part, rows, :] for part in range(3)]

        def level_term(level, start, i, c):
            dilation = 2**level
            at = start + (i * (CLASSES // dilation) + c // dilation) * RUN
            rows = slice(at, at + RUN)
            if level == 1:
                m, a, l = (res1[h % 2, part, rows, :] for part in range(3))
            else:
                m, a, l = res_m[rows, :], res_a[rows, :], res_l[rows, :]
            return jnp.where(shifts[level - 1] == c % dilation, m, NEG), a, l

        def levels23(slots):
            parts2 = scores2()
            parts3 = scores3(slots)
            keep(R2, N2, *softmax_parts(parts2))
            keep(R3, N3, *softmax_parts(parts3))

        @pl.when(y == 0)
        def _():
            levels23(1)
        @pl.when(y > 0)
        def _():
            levels23(7)
        @pl.when(y % 2 == 1)
        def _():
            join_far(h)
        for i in range(TOK // QUARTER):
            for c in range(CLASSES):
                terms = [base_term(i, c)]
                for level, start in ((1, 0), (2, R2), (3, R3)):
                    terms.append(level_term(level, start, i, c))
                _, num, den = joined(terms)
                att[h, i, c * RUN : (c + 1) * RUN, :] = (num / den).astype(BF16)
        for step in (2, 1, 3):
            send_att(h, step).start()
        abuf[x * HEADS_HERE + h] = att[h, x]

    def one_step(step, carry):
        h = step - 1
        @pl.when(step < HEADS_HERE)
        def _():
            level0(step)
        @pl.when(step == 2)
        def _():
            w_copy.start()
        @pl.when(step >= 2)
        def _():
            pass_near(h - 1)
        @pl.when((h >= 0) & (h < HEADS_HERE))
        def _():
            level1(h)
            pass_far(h)
            send2_partner(h).wait_recv()
            @pl.when(y % 2 == 0)
            def _():
                far(h)
        @pl.when(step == 0)
        def _():
            clear()
        @pl.when(step >= 2)
        def _():
            rest(h - 1)
        return carry

    lax.fori_loop(0, HEADS_HERE + 2, one_step, 0)

    w_copy.wait()

    def wait_att(h, carry):
        for step in range(1, 4):
            source = (x + 4 - step) % 4
            remote(
                att.at[h, 0], abuf.at[source * HEADS_HERE + h], sa.at[h, step], ra.at[h, step], ctx, (x + step) % 4
            ).wait_recv()
        return carry

    unperm = unperm_ref[...]
    lax.fori_loop(0, HEADS_HERE - 1, wait_att, 0)
    for g in range(4):
        block = jnp.concatenate([abuf[4 * g + i] for i in range(3)], axis=1)
        ap[:, g * 384 : (g + 1) * 384] = jnp.dot(unperm, block, preferred_element_type=F32).astype(BF16)

    def project_first(n, carry):
        at = pl.multiple_of(n * 512, 512)
        weight = jnp.concatenate([w_vm[g * 512 : g * 512 + 384, pl.ds(at, 512)] for g in range(4)], axis=0)
        total[:, pl.ds(at, 512)] = jnp.dot(ap[:, :1536], weight, preferred_element_type=F32)
        return carry

    lax.fori_loop(0, 4, project_first, 0)
    wait_att(HEADS_HERE - 1, 0)
    block = jnp.concatenate([abuf[4 * g + 3] for g in range(4)], axis=1)
    ap[:, 1536:] = jnp.dot(unperm, block, preferred_element_type=F32).astype(BF16)

    def project_last(n, carry):
        at = pl.multiple_of(n * 512, 512)
        weight = jnp.concatenate([w_vm[g * 512 + 384 : g * 512 + 512, pl.ds(at, 512)] for g in range(4)], axis=0)
        out_ref[:, pl.ds(at, 512)] = (
            total[:, pl.ds(at, 512)] + jnp.dot(ap[:, 1536:], weight, preferred_element_type=F32)
        ).astype(BF16)
        return carry

    lax.fori_loop(0, 4, project_last, 0)

    def wait_sends(h, carry):
        @pl.when(y == 0)
        def _():
            send3_y(h, 3).wait_send()
            forward3_up(h).wait_send()
        @pl.when(y == 1)
        def _():
            send3_via(h).wait_send()
        @pl.when(y == 3)
        def _():
            forward3_down(h).wait_send()
        @pl.when(y <= 2)
        def _():
            send3_y(h, 1).wait_send()
        for step in (1, 2, 3):
            @pl.when(y >= step)
            def _():
                relay3(h, step).wait_send()
            send_att(h, step).wait_send()
        @pl.when(y % 2 == 0)
        def _():
            send_far(h).wait_send()
            send_stat(h).wait_send()
        @pl.when(y % 2 == 1)
        def _():
            send_q(h).wait_send()
        send2_partner(h).wait_send()
        @pl.when(core == 0)
        def _():
            send1(h).wait_send()
            send3_partner(h).wait_send()
        return carry

    lax.fori_loop(0, HEADS_HERE, wait_sends, 0)


def positions(level):
    row = np.arange(QUARTER)
    if level == 0:
        c, j = row // RUN, row % RUN
        return CLASSES * j + c
    runs = CLASSES // 2**level
    block, b, j = row // (runs * RUN), row // RUN % runs, row % RUN
    return block * runs * RUN + runs * j + b


def body(queries, keys, values, offsets, out_weight):
    order = class_order(SUB)
    perm = jnp.asarray(np.eye(SUB)[order], BF16)
    unperm = jnp.asarray(np.eye(QUARTER)[class_order(QUARTER)].T, BF16)
    place = [positions(level) for level in range(3)]
    pq = [jnp.asarray(np.repeat(p[:, None], DH, 1), jnp.int32) for p in place]
    pk = [jnp.asarray(p[None, :], jnp.int32) for p in place]
    vm = pl.BlockSpec(memory_space=pltpu.VMEM)
    hbm = pl.BlockSpec(memory_space=pl.ANY)
    dma = pltpu.SemaphoreType.DMA
    return pl.pallas_call(
        main_kernel,
        in_specs=[pl.BlockSpec(memory_space=pltpu.SMEM)] + [hbm] * 4 + [vm] * 8,
        out_specs=vm,
        out_shape=jax.ShapeDtypeStruct((QUARTER, 2048), BF16),
        scratch_shapes=[
            pltpu.VMEM((HEADS_HERE, 3, TOK, DH), BF16),
            pltpu.VMEM((HEADS_HERE, ROWS, DH), BF16),
            pltpu.VMEM((HEADS_HERE, 2 * N1, DH), BF16),
            pltpu.VMEM((HEADS_HERE, 2 * N2, DH), BF16),
            pltpu.VMEM((7, HEADS_HERE, 2 * N3, DH), BF16),
            pltpu.VMEM((HEADS_HERE, 2 * N3, DH), BF16),
            pltpu.VMEM((HEADS_HERE, N2, DH), BF16),
            pltpu.VMEM((HEADS_HERE, N2, DH), BF16),
            pltpu.VMEM((HEADS_HERE, 16, N2), F32),
            pltpu.VMEM((HEADS_HERE, N2, DH), BF16),
            pltpu.VMEM((HEADS_HERE, 16, N2), F32),
            pltpu.VMEM((2048, 2048), BF16),
            pltpu.VMEM((16, QUARTER, DH), BF16),
            pltpu.VMEM((HEADS_HERE, 4, QUARTER, DH), BF16),
            pltpu.VMEM((QUARTER, 2048), BF16),
            pltpu.VMEM((QUARTER, 2048), F32),
            pltpu.VMEM((3, 3, TOK, DH), F32),
            pltpu.VMEM((2, 3, N1, DH), F32),
            pltpu.VMEM((RES, DH), F32),
            pltpu.VMEM((RES, DH), F32),
            pltpu.VMEM((RES, DH), F32),
            dma((4, 3)), dma,
            dma((4,)), dma((4,)), dma((4,)), dma((4,)), dma((4,)), dma((4, 8)), dma((4,)), dma((4, 4)),
            dma((4,)), dma((4,)), dma((4,)), dma((4,)), dma((4,)),
            dma((4,)), dma((4, 4)), dma((4, 4)), dma((4,)), dma((4, 4)),
        ],
        compiler_params=pltpu.CompilerParams(
            collective_id=0, has_side_effects=True, vmem_limit_bytes=62 * 2**20
        ),
        name="attend",
    )(offsets, queries, keys, values, out_weight, perm, unperm, *pq, *pk)


def solution(mesh):
    placed = (P("ctx", "head"), P("ctx", "head"), P("ctx", "head"), P(), P())
    return jax.shard_map(
        body, mesh=mesh, in_specs=placed, out_specs=P(("ctx", "head"), None), check_vma=False
    )
```

```python
import math

import jax
import jax.numpy as jnp
import numpy as np
from jax import lax
from jax.experimental import pallas as pl
from jax.experimental.pallas import tpu as pltpu
from jax.sharding import PartitionSpec as P

DH = 128
LEVELS = 4
CLASSES = 8
HEADS_HERE = 4
TOK = 1536
QUARTER = 384
RUN = QUARTER // CLASSES
SUB = 128
NEG = -1e30
SCALE = math.log2(math.e) / math.sqrt(DH)
MESH = pl.DeviceIdType.MESH
F32 = jnp.float32
BF16 = jnp.bfloat16

QC, KC, VC = 0, TOK, 2 * TOK
N1, N2, N3 = TOK // 2, TOK // 4, TOK // 8
Q1 = 3 * TOK
Q2 = Q1 + N1
Q3 = Q2 + N2
K1 = Q3 + N3
V1 = K1 + N1
K2 = V1 + N1
V2 = K2 + N2
K3 = V2 + N2
V3 = K3 + N3
ROWS = V3 + N3

R2, R3 = 0, N2
RES = N2 + N3


def class_order(tokens):
    return np.arange(tokens).reshape(tokens // CLASSES, CLASSES).T.reshape(-1)


def scores_of(q, k):
    return lax.dot_general(q, k, (((1,), (1,)), ((), ())), preferred_element_type=F32)


def softmax_parts(parts):
    top = None
    for s, _, valid in parts:
        high = jnp.max(s, axis=1, keepdims=True)
        if valid is not None:
            high = jnp.where(valid, high, NEG)
        top = high if top is None else jnp.maximum(top, high)
    weights, values = [], []
    for s, v, valid in parts:
        if valid is None:
            base = top
        else:
            base = jnp.where(valid, top, -NEG)
        weights.append(jnp.exp2((s - base) * SCALE).astype(BF16))
        values.append(jnp.concatenate([v, jnp.ones(v.shape, BF16)], axis=1))
    out = jnp.dot(
        jnp.concatenate(weights, axis=1), jnp.concatenate(values, axis=0), preferred_element_type=F32
    )
    return top, out


def pipelined(tiles):
    parts = tiles[0][0]()
    for at, (_, finish) in enumerate(tiles):
        ahead = tiles[at + 1][0]() if at + 1 < len(tiles) else None
        finish(*softmax_parts(parts))
        parts = ahead


def main_kernel(
    off_ref, q_hbm, k_hbm, v_hbm, w_hbm, perm_ref, unperm_ref, pq0, pq1, pq2, pk0, pk1, pk2, out_ref,
    raw, qkv, kv1, kv2, kv3, passing, qfar, farout, farstat, gota, gots, w_vm, abuf, att, ap, total, res0, res1, res_m, res_l, res_a,
    load_sem, w_sem, r1, r2, rq, rfa, rfs, r3, rp, ra, s1, s2p, sq, sfa, sfs, s3p, s3y, s3r, s3f, sa,
):
    ctx = lax.axis_index("ctx")
    x = lax.axis_index("head")
    core = ctx % 2
    y = (ctx // 2) % 4
    p8 = ctx % 8
    partner = ctx + 1 - 2 * core

    def at_y(step):
        return ctx + 2 * ((y + step) % 4 - y)

    def load(h, which):
        source = (q_hbm, k_hbm, v_hbm)[which]
        return pltpu.make_async_copy(
            source.at[:, pl.ds(h * DH, DH)], raw.at[h, which], load_sem.at[h, which]
        )

    w_copy = pltpu.make_async_copy(w_hbm, w_vm, w_sem)
    for h in range(HEADS_HERE):
        for which in range(3):
            load(h, which).start()

    barrier = pltpu.get_barrier_semaphore()
    pl.semaphore_signal(barrier, inc=1, device_id={"ctx": partner, "head": x}, device_id_type=MESH)
    for step in range(1, 4):
        pl.semaphore_signal(barrier, inc=1, device_id={"ctx": at_y(step), "head": x}, device_id_type=MESH)
        pl.semaphore_signal(barrier, inc=1, device_id={"ctx": ctx, "head": (x + step) % 4}, device_id_type=MESH)
    pl.semaphore_wait(barrier, 7)

    def remote(source, target, send, recv, to_ctx, to_head):
        return pltpu.make_async_remote_copy(
            src_ref=source, dst_ref=target, send_sem=send, recv_sem=recv,
            device_id={"ctx": to_ctx, "head": to_head}, device_id_type=MESH,
        )

    def send1(h):
        return remote(qkv.at[h, pl.ds(K1, 2 * N1)], kv1.at[h], s1.at[h], r1.at[h], partner, x)

    def send2_partner(h):
        return remote(qkv.at[h, pl.ds(K2, 2 * N2)], kv2.at[h], s2p.at[h], r2.at[h], partner, x)

    def send_q(h):
        return remote(qkv.at[h, pl.ds(Q2, N2)], qfar.at[h], sq.at[h], rq.at[h], at_y(3), x)

    def send_far(h):
        return remote(farout.at[h], gota.at[h], sfa.at[h], rfa.at[h], at_y(1), x)

    def send_stat(h):
        return remote(farstat.at[h], gots.at[h], sfs.at[h], rfs.at[h], at_y(1), x)

    def send3_partner(h):
        return remote(qkv.at[h, pl.ds(K3, 2 * N3)], kv3.at[0, h], s3p.at[h], r3.at[h, 1], partner, x)

    def send3_y(h, step):
        return remote(
            qkv.at[h, pl.ds(K3, 2 * N3)], kv3.at[2 * step - 1, h], s3y.at[h, step],
            r3.at[h, 2 * step], at_y(step), x,
        )

    def send3_via(h):
        return remote(qkv.at[h, pl.ds(K3, 2 * N3)], passing.at[h], s3y.at[h, 2], rp.at[h], at_y(3), x)

    def forward3_up(h):
        return remote(passing.at[h], kv3.at[3, h], s3f.at[h], r3.at[h, 4], at_y(3), x)

    def forward3_down(h):
        return remote(kv3.at[5, h], kv3.at[3, h], s3f.at[h], r3.at[h, 4], at_y(3), x)

    def relay3(h, step):
        slot = 2 * step + 1 - 2 * core
        return remote(
            kv3.at[2 * step - 1, h], kv3.at[slot - 1, h], s3r.at[h, step], r3.at[h, slot], partner, x
        )

    def send_att(h, step):
        to = (x + step) % 4
        return remote(att.at[h, to], abuf.at[x * HEADS_HERE + h], sa.at[h, step], ra.at[h, step], ctx, to)

    def start_sends(h, carry):
        @pl.when(y % 2 == 1)
        def _():
            send_q(h).start()
        @pl.when(y == 0)
        def _():
            send3_y(h, 3).start()
        @pl.when(y == 1)
        def _():
            send3_via(h).start()
        @pl.when(y <= 2)
        def _():
            send3_y(h, 1).start()
        send2_partner(h).start()
        @pl.when(core == 0)
        def _():
            send1(h).start()
            send3_partner(h).start()
        return carry

    def pick(h, carry):
        head = x * HEADS_HERE + h
        perm = perm_ref[...]
        run_sub = SUB // CLASSES
        for which in range(3):
            pltpu.make_async_copy(q_hbm.at[:, pl.ds(0, DH)], raw.at[h, which], load_sem.at[h, which]).wait()
        pieces = [(which, base, sub) for sub in range(TOK // SUB) for which, base in enumerate((QC, KC, VC))]
        for first in range(0, len(pieces), 6):
            group = pieces[first : first + 6]
            block = jnp.concatenate(
                [raw[h, which, sub * SUB : (sub + 1) * SUB, :] for which, _, sub in group], axis=1
            )
            moved = jnp.dot(perm, block, preferred_element_type=F32).astype(BF16)
            for at, (_, base, sub) in enumerate(group):
                quarter, part = divmod(sub, QUARTER // SUB)
                for c in range(CLASSES):
                    row = base + quarter * QUARTER + c * RUN + part * run_sub
                    qkv[h, row : row + run_sub, :] = moved[
                        c * run_sub : (c + 1) * run_sub, at * DH : (at + 1) * DH
                    ]
        for base, targets in ((QC, (Q1, Q2, Q3)), (KC, (K1, K2, K3)), (VC, (V1, V2, V3))):
            for level in range(1, LEVELS):
                dilation = 2**level
                runs = CLASSES // dilation
                shift = off_ref[level - 1, head]
                for quarter in range(TOK // QUARTER):
                    for b in range(runs):
                        row = base + quarter * QUARTER + dilation * b * RUN
                        to = targets[level - 1] + (quarter * runs + b) * RUN
                        found = qkv[h, row : row + RUN, :]
                        for c in range(1, dilation):
                            other = qkv[h, row + c * RUN : row + c * RUN + RUN, :]
                            found = jnp.where(shift == c, other, found)
                        qkv[h, to : to + RUN, :] = found
        @pl.when(h > 0)
        def _():
            start_sends(h - 1, 0)
        return carry

    lax.fori_loop(0, HEADS_HERE, pick, 0)
    start_sends(HEADS_HERE - 1, 0)

    def clear():
        @pl.when(core == 0)
        def _():
            kv1[...] = jnp.zeros(kv1.shape, BF16)
        for slot in range(1, 8):
            @pl.when((slot > p8) & ((y > 0) | (slot == 1)))
            def _():
                kv3[slot - 1] = jnp.zeros(kv3.shape[1:], BF16)

    def own(h, row, count):
        return qkv[h, row : row + count, :]

    def keep(row, count, top, out):
        res_m[row : row + count, :] = jnp.broadcast_to(top, (count, DH))
        res_a[row : row + count, :] = out[:, :DH]
        res_l[row : row + count, :] = out[:, DH:]

    def masked(s, pq, pk):
        seen = jnp.concatenate([pq[...]] * (QUARTER // DH), axis=1) >= pk[...]
        return jnp.where(seen, s, NEG)

    def level0(h):
        def tile(i):
            def scores():
                q = own(h, QC + i * QUARTER, QUARTER)
                near = masked(scores_of(q, own(h, KC + i * QUARTER, QUARTER)), pq0, pk0)
                parts = [(near, own(h, VC + i * QUARTER, QUARTER), None)]
                if i:
                    parts.append((scores_of(q, own(h, KC, i * QUARTER)), own(h, VC, i * QUARTER), None))
                return parts

            def finish(top, out):
                rows = slice(i * QUARTER, (i + 1) * QUARTER)
                res0[h % 3, 0, rows, :] = jnp.broadcast_to(top, (QUARTER, DH))
                res0[h % 3, 1, rows, :] = out[:, :DH]
                res0[h % 3, 2, rows, :] = out[:, DH:]

            return scores, finish

        pipelined([tile(i) for i in (3, 2, 1, 0)])

    def pass_far(h):
        @pl.when(y == 0)
        def _():
            send3_via(h).wait_recv()
            forward3_up(h).start()
        @pl.when(y == 3)
        def _():
            send3_y(h, 3).wait_recv()
            forward3_down(h).start()
            relay3(h, 3).start()

    def pass_near(h):
        for step in (1, 2):
            @pl.when(y >= step)
            def _():
                send3_y(h, step).wait_recv()
                relay3(h, step).start()

    def level1(h):
        @pl.when(core == 1)
        def _():
            send1(h).wait_recv()
        def tile(i):
            def scores():
                q = own(h, Q1 + i * QUARTER, QUARTER)
                near = masked(scores_of(q, own(h, K1 + i * QUARTER, QUARTER)), pq1, pk1)
                parts = [(near, own(h, V1 + i * QUARTER, QUARTER), None)]
                if i:
                    parts.append((scores_of(q, own(h, K1, i * QUARTER)), own(h, V1, i * QUARTER), None))
                parts.append((scores_of(q, kv1[h, :N1]), kv1[h, N1:], core == 1))
                return parts

            def finish(top, out):
                rows = slice(i * QUARTER, (i + 1) * QUARTER)
                res1[h % 2, 0, rows, :] = jnp.broadcast_to(top, (QUARTER, DH))
                res1[h % 2, 1, rows, :] = out[:, :DH]
                res1[h % 2, 2, rows, :] = out[:, DH:]

            return scores, finish

        pipelined([tile(1), tile(0)])

    def far(h):
        send_q(h).wait_recv()
        q = qfar[h]
        top, out = softmax_parts([
            (scores_of(q, own(h, K2, N2)), own(h, V2, N2), None),
            (scores_of(q, kv2[h, :N2]), kv2[h, N2:], None),
        ])
        farout[h] = out[:, :DH].astype(BF16)
        lane = lax.broadcasted_iota(jnp.int32, (N2, DH), 1)
        both = jnp.where(lane < DH // 2, jnp.broadcast_to(top, (N2, DH)), out[:, DH:]).T
        farstat[h, :8, :] = both[:8, :]
        farstat[h, 8:, :] = both[DH // 2 : DH // 2 + 8, :]
        send_far(h).start()
        send_stat(h).start()

    def join_far(h):
        send_far(h).wait_recv()
        send_stat(h).wait_recv()
        m_far = jnp.broadcast_to(gots[h, 0:1, :], (DH, N2)).T
        l_far = jnp.broadcast_to(gots[h, 8:9, :], (DH, N2)).T
        rows = slice(R2, R2 + N2)
        m = res_m[rows, :]
        high = jnp.maximum(m, m_far)
        here = jnp.exp2((m - high) * SCALE)
        there = jnp.exp2((m_far - high) * SCALE)
        res_m[rows, :] = high
        res_l[rows, :] = here * res_l[rows, :] + there * l_far
        res_a[rows, :] = here * res_a[rows, :] + there * gota[h].astype(F32)

    def rest(h):
        for slot in (1, 3, 5, 7):
            @pl.when(slot <= p8)
            def _():
                remote(kv3.at[0, h], kv3.at[slot - 1, h], s3p.at[h], r3.at[h, slot], partner, x).wait_recv()
        def scores2():
            q = own(h, Q2, N2)
            parts = [(masked(scores_of(q, own(h, K2, N2)), pq2, pk2), own(h, V2, N2), None)]
            parts.append((scores_of(q, kv2[h, :N2]), kv2[h, N2:], core == 1))
            return parts

        def scores3(slots):
            width = (slots + 1) * N3
            keys = jnp.concatenate([own(h, K3, N3)] + [kv3[d, h, :N3] for d in range(slots)], axis=0)
            vals = jnp.concatenate([own(h, V3, N3)] + [kv3[d, h, N3:] for d in range(slots)], axis=0)
            column = lax.broadcasted_iota(jnp.int32, (1, width), 1)
            least = jnp.where(column < N3, column, jnp.where(column < N3 * (p8 + 1), -1, TOK))
            row = lax.broadcasted_iota(jnp.int32, (N3, width), 0)
            return [(jnp.where(row >= least, scores_of(own(h, Q3, N3), keys), NEG), vals, None)]

        head = x * HEADS_HERE + h
        shifts = [off_ref[level - 1, head] for level in range(1, LEVELS)]

        def joined(terms):
            high = terms[0][0]
            for m, _, _ in terms[1:]:
                high = jnp.maximum(high, m)
            num = den = None
            for m, a, l in terms:
                f = jnp.exp2((m - high) * SCALE)
                num = f * a if num is None else num + f * a
                den = f * l if den is None else den + f * l
            return high, num, den

        def base_term(i, c):
            rows = slice(i * QUARTER + c * RUN, i * QUARTER + c * RUN + RUN)
            return [res0[h % 3, part, rows, :] for part in range(3)]

        def level_term(level, start, i, c):
            dilation = 2**level
            at = start + (i * (CLASSES // dilation) + c // dilation) * RUN
            rows = slice(at, at + RUN)
            if level == 1:
                m, a, l = (res1[h % 2, part, rows, :] for part in range(3))
            else:
                m, a, l = res_m[rows, :], res_a[rows, :], res_l[rows, :]
            return jnp.where(shifts[level - 1] == c % dilation, m, NEG), a, l

        def levels23(slots):
            parts2 = scores2()
            parts3 = scores3(slots)
            keep(R2, N2, *softmax_parts(parts2))
            keep(R3, N3, *softmax_parts(parts3))

        @pl.when(y == 0)
        def _():
            levels23(1)
        @pl.when(y > 0)
        def _():
            levels23(7)
        @pl.when(y % 2 == 1)
        def _():
            join_far(h)
        for i in range(TOK // QUARTER):
            for c in range(CLASSES):
                terms = [base_term(i, c)]
                for level, start in ((1, 0), (2, R2), (3, R3)):
                    terms.append(level_term(level, start, i, c))
                _, num, den = joined(terms)
                att[h, i, c * RUN : (c + 1) * RUN, :] = (num / den).astype(BF16)
        for step in (2, 1, 3):
            send_att(h, step).start()
        abuf[x * HEADS_HERE + h] = att[h, x]

    def one_step(step, carry):
        h = step - 1
        @pl.when(step < HEADS_HERE)
        def _():
            level0(step)
        @pl.when(step == 2)
        def _():
            w_copy.start()
        @pl.when(step >= 2)
        def _():
            pass_near(h - 1)
        @pl.when((h >= 0) & (h < HEADS_HERE))
        def _():
            level1(h)
            pass_far(h)
            send2_partner(h).wait_recv()
            @pl.when(y % 2 == 0)
            def _():
                far(h)
        @pl.when(step == 0)
        def _():
            clear()
        @pl.when(step >= 2)
        def _():
            rest(h - 1)
        return carry

    lax.fori_loop(0, HEADS_HERE + 2, one_step, 0)

    w_copy.wait()

    def wait_att(h, carry):
        for step in range(1, 4):
            source = (x + 4 - step) % 4
            remote(
                att.at[h, 0], abuf.at[source * HEADS_HERE + h], sa.at[h, step], ra.at[h, step], ctx, (x + step) % 4
            ).wait_recv()
        return carry

    unperm = unperm_ref[...]
    lax.fori_loop(0, HEADS_HERE - 1, wait_att, 0)
    block = jnp.concatenate([abuf[4 * g + i] for g in range(4) for i in range(3)], axis=1)
    ap[:, :1536] = jnp.dot(unperm, block, preferred_element_type=F32).astype(BF16)

    def project_first(n, carry):
        at = pl.multiple_of(n * 512, 512)
        weight = jnp.concatenate([w_vm[g * 512 : g * 512 + 384, pl.ds(at, 512)] for g in range(4)], axis=0)
        total[:, pl.ds(at, 512)] = jnp.dot(ap[:, :1536], weight, preferred_element_type=F32)
        return carry

    lax.fori_loop(0, 4, project_first, 0)
    wait_att(HEADS_HERE - 1, 0)
    block = jnp.concatenate([abuf[4 * g + 3] for g in range(4)], axis=1)
    ap[:, 1536:] = jnp.dot(unperm, block, preferred_element_type=F32).astype(BF16)

    def project_last(n, carry):
        at = pl.multiple_of(n * 512, 512)
        weight = jnp.concatenate([w_vm[g * 512 + 384 : g * 512 + 512, pl.ds(at, 512)] for g in range(4)], axis=0)
        out_ref[:, pl.ds(at, 512)] = (
            total[:, pl.ds(at, 512)] + jnp.dot(ap[:, 1536:], weight, preferred_element_type=F32)
        ).astype(BF16)
        return carry

    lax.fori_loop(0, 4, project_last, 0)

    def wait_sends(h, carry):
        @pl.when(y == 0)
        def _():
            send3_y(h, 3).wait_send()
            forward3_up(h).wait_send()
        @pl.when(y == 1)
        def _():
            send3_via(h).wait_send()
        @pl.when(y == 3)
        def _():
            forward3_down(h).wait_send()
        @pl.when(y <= 2)
        def _():
            send3_y(h, 1).wait_send()
        for step in (1, 2, 3):
            @pl.when(y >= step)
            def _():
                relay3(h, step).wait_send()
            send_att(h, step).wait_send()
        @pl.when(y % 2 == 0)
        def _():
            send_far(h).wait_send()
            send_stat(h).wait_send()
        @pl.when(y % 2 == 1)
        def _():
            send_q(h).wait_send()
        send2_partner(h).wait_send()
        @pl.when(core == 0)
        def _():
            send1(h).wait_send()
            send3_partner(h).wait_send()
        return carry

    lax.fori_loop(0, HEADS_HERE, wait_sends, 0)


def positions(level):
    row = np.arange(QUARTER)
    if level == 0:
        c, j = row // RUN, row % RUN
        return CLASSES * j + c
    runs = CLASSES // 2**level
    block, b, j = row // (runs * RUN), row // RUN % runs, row % RUN
    return block * runs * RUN + runs * j + b


def body(queries, keys, values, offsets, out_weight):
    order = class_order(SUB)
    perm = jnp.asarray(np.eye(SUB)[order], BF16)
    unperm = jnp.asarray(np.eye(QUARTER)[class_order(QUARTER)].T, BF16)
    place = [positions(level) for level in range(3)]
    pq = [jnp.asarray(np.repeat(p[:, None], DH, 1), jnp.int32) for p in place]
    pk = [jnp.asarray(p[None, :], jnp.int32) for p in place]
    vm = pl.BlockSpec(memory_space=pltpu.VMEM)
    hbm = pl.BlockSpec(memory_space=pl.ANY)
    dma = pltpu.SemaphoreType.DMA
    return pl.pallas_call(
        main_kernel,
        in_specs=[pl.BlockSpec(memory_space=pltpu.SMEM)] + [hbm] * 4 + [vm] * 8,
        out_specs=vm,
        out_shape=jax.ShapeDtypeStruct((QUARTER, 2048), BF16),
        scratch_shapes=[
            pltpu.VMEM((HEADS_HERE, 3, TOK, DH), BF16),
            pltpu.VMEM((HEADS_HERE, ROWS, DH), BF16),
            pltpu.VMEM((HEADS_HERE, 2 * N1, DH), BF16),
            pltpu.VMEM((HEADS_HERE, 2 * N2, DH), BF16),
            pltpu.VMEM((7, HEADS_HERE, 2 * N3, DH), BF16),
            pltpu.VMEM((HEADS_HERE, 2 * N3, DH), BF16),
            pltpu.VMEM((HEADS_HERE, N2, DH), BF16),
            pltpu.VMEM((HEADS_HERE, N2, DH), BF16),
            pltpu.VMEM((HEADS_HERE, 16, N2), F32),
            pltpu.VMEM((HEADS_HERE, N2, DH), BF16),
            pltpu.VMEM((HEADS_HERE, 16, N2), F32),
            pltpu.VMEM((2048, 2048), BF16),
            pltpu.VMEM((16, QUARTER, DH), BF16),
            pltpu.VMEM((HEADS_HERE, 4, QUARTER, DH), BF16),
            pltpu.VMEM((QUARTER, 2048), BF16),
            pltpu.VMEM((QUARTER, 2048), F32),
            pltpu.VMEM((3, 3, TOK, DH), F32),
            pltpu.VMEM((2, 3, N1, DH), F32),
            pltpu.VMEM((RES, DH), F32),
            pltpu.VMEM((RES, DH), F32),
            pltpu.VMEM((RES, DH), F32),
            dma((4, 3)), dma,
            dma((4,)), dma((4,)), dma((4,)), dma((4,)), dma((4,)), dma((4, 8)), dma((4,)), dma((4, 4)),
            dma((4,)), dma((4,)), dma((4,)), dma((4,)), dma((4,)),
            dma((4,)), dma((4, 4)), dma((4, 4)), dma((4,)), dma((4, 4)),
        ],
        compiler_params=pltpu.CompilerParams(
            collective_id=0, has_side_effects=True, vmem_limit_bytes=62 * 2**20
        ),
        name="attend",
    )(offsets, queries, keys, values, out_weight, perm, unperm, *pq, *pk)


def solution(mesh):
    placed = (P("ctx", "head"), P("ctx", "head"), P("ctx", "head"), P(), P())
    return jax.shard_map(
        body, mesh=mesh, in_specs=placed, out_specs=P(("ctx", "head"), None), check_vma=False
    )
```
